32 devices in a mesh: ctx: 16 (over z, y, core), tp: 2 (over x).
Axes of the slice: x: 2, y: 2, z: 4, core: 2. Of those that a mesh axis runs over, the one named last changes fastest.
Arguments:
- query: bfloat16 [4096, 8192], P('ctx', 'tp'), may hold values from -20 to 20
- key: bfloat16 [4096, 1024], P('ctx', 'tp'), may hold values from -4 to 4
- value: bfloat16 [4096, 1024], P('ctx', 'tp'), may hold values from -6 to 6
- output_cotangent: bfloat16 [4096, 8192], P('ctx', 'tp'), may hold values from -6 to 6
- parents: int32 [32], replicated, may hold values from 0 to 30, as said below
Outputs:
- attn_out: bfloat16 [4096, 8192], P('ctx', 'tp')
- grad_query: bfloat16 [4096, 8192], P('ctx', 'tp')
- grad_key: bfloat16 [4096, 1024], P('ctx', 'tp')
- grad_value: bfloat16 [4096, 1024], P('ctx', 'tp')
The draws below stay inside these ranges and needn't reach their ends.
Inputs may be any that keep to these rules, and one draw needn't show every extreme that they name: parents[0] = 0 and parents[b] < b for every other block b; every ancestor of a block, other than block 0, lies on the block's own index of ctx or on one of the 3 indices before it. In every draw, the blocks of index 3 of ctx, and of every index of ctx that is a positive multiple of 4, read ancestors held by each of the 3 indices before it.
All inputs are finite; a program needn't handle non-finite values.
Results may differ from the reference program's by a relative error of at most 0.0091.
Values may be sent and summed in bfloat16 or wider, within the bound.
No kernel may reach another device: no remote copies, remote signals or barrier semaphores. Data moves between devices by JAX's collectives and lax.ppermute only.
A program may use at most 128 MiB of HBM per device.

```python
import math
import jax
import jax.numpy as jnp
from jax import lax

QUERY_HEAD_COUNT = 64
KEY_VALUE_HEADS = 8
HEAD_WIDTH = 128
SHARD_TOKENS = 256
BLOCK_TOKENS = 128
HOPS = 3
WINDOW_TOKENS = 4096
N_CTX = 16


def shared_keys(seed_generator):
    seed_random_key = jax.random.fold_in(seed_generator, 101)
    dense_table = jax.random.truncated_normal(seed_random_key, -4.0, 4.0, (WINDOW_TOKENS, KEY_VALUE_HEADS * HEAD_WIDTH), jnp.float32)
    return dense_table


def draw_key(key, part):
    return shared_keys(key).astype(jnp.bfloat16)


def draw_query(key, part):
    result = jax.random.truncated_normal(jax.random.fold_in(key, 202), -4.0, 4.0, (WINDOW_TOKENS, QUERY_HEAD_COUNT * HEAD_WIDTH), jnp.float32)
    return result.astype(jnp.bfloat16)


def draw_parents(key, part):
    block_count = WINDOW_TOKENS // BLOCK_TOKENS
    blocks_here = SHARD_TOKENS // BLOCK_TOKENS
    period = HOPS + 1
    block_ids = jnp.arange(block_count, dtype=jnp.int32)
    device_ids = block_ids // blocks_here
    slot_ids = block_ids % blocks_here
    choice_roll = jax.random.randint(jax.random.fold_in(key, 11), (block_count,), 0, 3)
    spine_ok = (device_ids >= 1) & ((device_ids % period != 1) | (device_ids == 1))
    spine_parent = jnp.where(spine_ok, device_ids * blocks_here - 1, 0)
    other_parent = jnp.where(choice_roll == 0, 0, jnp.where((choice_roll == 1) & (slot_ids > 0), block_ids - 1, spine_parent))
    parent = jnp.where(slot_ids == blocks_here - 1, spine_parent, other_parent)
    parent = jnp.where(block_ids == block_count - 1, block_ids - 1, parent)
    parent = jnp.where(block_ids == 0, 0, parent)
    return parent.astype(jnp.int32)


def level_of(key, dims, split, smallest, high):
    def one(axis_at, blocks):
        draws = jax.random.uniform(jax.random.fold_in(jax.random.fold_in(key, 6), axis_at), (blocks,), jnp.float32, smallest / len(split), high / len(split))
        return jnp.repeat(jnp.exp(draws), dims[axis_at] // blocks).reshape((-1,) + (1,) * (len(dims) - axis_at - 1))

    factor_of = one(*split[0])
    for cut in split[1:]:
        factor_of = factor_of * one(*cut)
    return factor_of


def centred(key, shape, spread, reach, pieces=(), kind=jnp.bfloat16):
    level = level_of(key, shape, pieces, -0.22, 0.18) if pieces else 1.0
    drawn = jax.random.normal(key, shape, jnp.float32) * spread * level
    return jnp.minimum(jnp.maximum(drawn, -reach), reach).astype(kind)


def setup_inputs(seed: int = 0) -> dict:
    keys = jax.random.split(jax.random.key(seed), 6)
    query = draw_query(jax.random.fold_in(keys[5], 71), 0)
    key = draw_key(jax.random.fold_in(keys[5], 71), 0)
    value = centred(keys[2], (WINDOW_TOKENS, KEY_VALUE_HEADS * HEAD_WIDTH), 1.0, 6.0, ((0, 16), (1, 2)))
    output_cotangent = centred(keys[3], (WINDOW_TOKENS, QUERY_HEAD_COUNT * HEAD_WIDTH), 1.0, 6.0, ((0, 16), (1, 2)))
    parents = draw_parents(jax.random.fold_in(keys[5], 71), 0)
    return dict(query=query, key=key, value=value, output_cotangent=output_cotangent, parents=parents)


def reference(query, key, value, output_cotangent, parents):
    block_count = parents.shape[0]
    block_ids = jnp.arange(block_count, dtype=jnp.int32)

    def climb_tree(state, unused):
        current, ancestry = state
        current = parents[current]
        ancestry = ancestry | (current[:, None] == block_ids[None, :])
        return ((current, ancestry), None)
    start_state = (block_ids, block_ids[:, None] == block_ids[None, :])
    (current, ancestry), unused = lax.scan(climb_tree, start_state, None, length=block_count)
    blocks_here = SHARD_TOKENS // BLOCK_TOKENS
    window_rows = (HOPS + 1) * SHARD_TOKENS
    key_slice = BLOCK_TOKENS + window_rows
    heads_per_group = QUERY_HEAD_COUNT // KEY_VALUE_HEADS
    score_scale = 1.0 / math.sqrt(HEAD_WIDTH)
    padding_rows = HOPS * SHARD_TOKENS
    padded_keys = jnp.concatenate([jnp.zeros((padding_rows, KEY_VALUE_HEADS * HEAD_WIDTH), key.dtype), key], axis=0)
    padded_values = jnp.concatenate([jnp.zeros((padding_rows, KEY_VALUE_HEADS * HEAD_WIDTH), value.dtype), value], axis=0)
    ancestry_pad = jnp.concatenate([jnp.zeros((block_count, HOPS * blocks_here), bool), ancestry], axis=1)

    def owner_step(carry, owner):
        key_acc, value_acc = carry
        first_row_index = owner * SHARD_TOKENS
        local_query = lax.dynamic_slice_in_dim(query, first_row_index, SHARD_TOKENS, 0).reshape(SHARD_TOKENS, KEY_VALUE_HEADS, heads_per_group, HEAD_WIDTH).astype(jnp.float32)
        local_gradient = lax.dynamic_slice_in_dim(output_cotangent, first_row_index, SHARD_TOKENS, 0).reshape(SHARD_TOKENS, KEY_VALUE_HEADS, heads_per_group, HEAD_WIDTH).astype(jnp.float32)
        windowed_keys = lax.dynamic_slice_in_dim(padded_keys, first_row_index, window_rows, 0)
        windowed_values = lax.dynamic_slice_in_dim(padded_values, first_row_index, window_rows, 0)
        key_rows_full = jnp.concatenate([key[:BLOCK_TOKENS], windowed_keys], axis=0).reshape(key_slice, KEY_VALUE_HEADS, HEAD_WIDTH).astype(jnp.float32)
        value_rows_full = jnp.concatenate([value[:BLOCK_TOKENS], windowed_values], axis=0).reshape(key_slice, KEY_VALUE_HEADS, HEAD_WIDTH).astype(jnp.float32)
        block_start = (owner * blocks_here).astype(jnp.int32)
        marks = lax.dynamic_slice(ancestry_pad, (block_start, block_start), (blocks_here, (HOPS + 1) * blocks_here))
        token_marks = jnp.repeat(jnp.repeat(marks, BLOCK_TOKENS, axis=0), BLOCK_TOKENS, axis=1)
        query_pos = owner * SHARD_TOKENS + jnp.arange(SHARD_TOKENS, dtype=jnp.int32)
        window_pos = (owner - HOPS) * SHARD_TOKENS + jnp.arange(window_rows, dtype=jnp.int32)
        root_pos = jnp.arange(BLOCK_TOKENS, dtype=jnp.int32)
        window_ok = token_marks & (window_pos >= BLOCK_TOKENS)[None, :] & (window_pos[None, :] <= query_pos[:, None])
        root_ok = root_pos[None, :] <= query_pos[:, None]
        visible = jnp.concatenate([root_ok, window_ok], axis=1)
        scores = jnp.einsum('tgrd,ugd->grtu', local_query, key_rows_full) * score_scale
        scores = jnp.where(visible, scores, -jnp.inf)
        row_max = lax.optimization_barrier(jnp.max(scores, axis=3, keepdims=True))
        row_total = lax.optimization_barrier(jnp.sum(jnp.exp(scores - row_max), axis=3, keepdims=True))
        log_total = row_max + jnp.log(row_total)
        probabilities = jnp.exp(scores - log_total)
        weights = probabilities.astype(jnp.bfloat16)
        attention_weights_full = weights.astype(jnp.float32)
        attended = jnp.einsum('grtu,ugd->tgrd', attention_weights_full, value_rows_full).astype(jnp.bfloat16)
        row_delta = lax.optimization_barrier(jnp.sum(local_gradient * attended.astype(jnp.float32), axis=3))
        grad_prob = jnp.einsum('tgrd,ugd->grtu', local_gradient, value_rows_full)
        dscore = (probabilities * (grad_prob - jnp.transpose(row_delta, (1, 2, 0))[..., None]) * score_scale).astype(jnp.bfloat16)
        score_gradient_full = dscore.astype(jnp.float32)
        grad_q = jnp.einsum('grtu,ugd->tgrd', score_gradient_full, key_rows_full).astype(jnp.bfloat16)
        key_gradient_terms = jnp.einsum('inxo,xinj->oij', score_gradient_full, local_query).reshape(key_slice, KEY_VALUE_HEADS * HEAD_WIDTH)
        value_gradient_terms = jnp.einsum('inxo,xinj->oij', attention_weights_full, local_gradient).reshape(key_slice, KEY_VALUE_HEADS * HEAD_WIDTH)
        key_acc = key_acc.at[padding_rows:padding_rows + BLOCK_TOKENS].add(key_gradient_terms[:BLOCK_TOKENS])
        value_acc = value_acc.at[padding_rows:padding_rows + BLOCK_TOKENS].add(value_gradient_terms[:BLOCK_TOKENS])
        key_old = lax.dynamic_slice_in_dim(key_acc, first_row_index, window_rows, 0)
        value_old = lax.dynamic_slice_in_dim(value_acc, first_row_index, window_rows, 0)
        key_acc = lax.dynamic_update_slice_in_dim(key_acc, key_old + key_gradient_terms[BLOCK_TOKENS:], first_row_index, 0)
        value_acc = lax.dynamic_update_slice_in_dim(value_acc, value_old + value_gradient_terms[BLOCK_TOKENS:], first_row_index, 0)
        outputs = (attended.reshape(SHARD_TOKENS, QUERY_HEAD_COUNT * HEAD_WIDTH), grad_q.reshape(SHARD_TOKENS, QUERY_HEAD_COUNT * HEAD_WIDTH))
        return ((key_acc, value_acc), outputs)
    initial_totals = jnp.zeros((padding_rows + WINDOW_TOKENS, KEY_VALUE_HEADS * HEAD_WIDTH), jnp.float32)
    (key_acc, value_acc), (attended_all, grad_q_all) = lax.scan(owner_step, (initial_totals, initial_totals), jnp.arange(N_CTX, dtype=jnp.int32))
    attn_out = attended_all.reshape(WINDOW_TOKENS, QUERY_HEAD_COUNT * HEAD_WIDTH)
    grad_query = grad_q_all.reshape(WINDOW_TOKENS, QUERY_HEAD_COUNT * HEAD_WIDTH)
    grad_key = key_acc[padding_rows:].astype(jnp.bfloat16)
    grad_value = value_acc[padding_rows:].astype(jnp.bfloat16)
    return (attn_out, grad_query, grad_key, grad_value)
```

```python
import functools
import math

import jax
import jax.numpy as jnp
from jax import lax
from jax.experimental import pallas as pl
from jax.experimental.pallas import tpu as pltpu
from jax.sharding import PartitionSpec as P

HEAD_WIDTH = 128
BLOCK_TOKENS = 128
HOPS = 3
CHUNK_HEADS = 4


def passed_along(array, by):
    devices = lax.axis_size("ctx")
    pairs = [(i, i + by) for i in range(devices) if 0 <= i + by < devices]
    return lax.ppermute(array, "ctx", pairs)


def tree_stages(devices):
    stages = []
    size = devices
    while size > 1:
        fan = 4 if size % 4 == 0 else (2 if size % 2 == 0 else size)
        size //= fan
        stages.append((size, fan))
    return stages


def spread_from_first(value):
    devices = lax.axis_size("ctx")
    held = jnp.where(lax.axis_index("ctx") == 0, value, 0).astype(value.dtype)
    for stride, fan in tree_stages(devices):
        arrived = [
            lax.ppermute(
                held, "ctx", [(i, i + j * stride) for i in range(0, devices, stride * fan)]
            )
            for j in range(1, fan)
        ]
        for piece in arrived:
            held = held + piece
    return held


def sum_to_first(terms):
    devices = lax.axis_size("ctx")
    total = terms.astype(jnp.float32)
    for stride, fan in reversed(tree_stages(devices)):
        sent = total.astype(jnp.bfloat16)
        for j in range(1, fan):
            total = total + lax.ppermute(
                sent, "ctx", [(i + j * stride, i) for i in range(0, devices, stride * fan)]
            ).astype(jnp.float32)
    return total


def export_kernel(blocks_here, parents_ref, choice_ref, reach_ref):
    block_count = parents_ref.shape[0]
    devices = block_count // blocks_here

    @pl.loop(0, block_count)
    def _(b):
        reach_ref[b] = b // blocks_here

    @pl.loop(0, block_count)
    def _(step):
        b = block_count - 1 - step
        up = parents_ref[b]
        reach_ref[up] = jnp.maximum(reach_ref[up], reach_ref[b])

    def visit(device, crowded):
        count = jnp.int32(0)
        choice = jnp.int32(0)
        for slot in range(blocks_here):
            block = device * blocks_here + slot
            read = ((reach_ref[block] > device) & (block > 0)).astype(jnp.int32)
            count = count + read
            choice = jnp.where(read > 0, slot, choice)
        choice_ref[device] = choice
        return jnp.maximum(crowded, count)

    choice_ref[devices] = lax.fori_loop(0, devices, visit, jnp.int32(0))


def exported_blocks(parents, blocks_here):
    block_count = parents.shape[0]
    return pl.pallas_call(
        functools.partial(export_kernel, blocks_here),
        out_shape=jax.ShapeDtypeStruct((block_count // blocks_here + 1,), jnp.int32),
        in_specs=[pl.BlockSpec(memory_space=pltpu.SMEM)],
        out_specs=pl.BlockSpec(memory_space=pltpu.SMEM),
        scratch_shapes=[pltpu.SMEM((block_count,), jnp.int32)],
        name="exported",
    )(parents)


NT = (((1,), (1,)), ((), ()))
NN = (((1,), (0,)), ((), ()))
TN = (((0,), (0,)), ((), ()))


def dot(a, b, dims):
    return lax.dot_general(a, b, dims, preferred_element_type=jnp.float32)


def attention_kernel(
    carried, blocks_here, heads_per_group, parents_ref, q_ref, do_ref, k_own, v_own, root_ref,
    *rest,
):
    pieces = rest[:HOPS]
    (out_ref, gq_ref, gown_ref, groot_ref) = rest[HOPS : HOPS + 4]
    gpieces = rest[HOPS + 4 : 2 * HOPS + 4]
    k_all, v_all, gk_acc, gv_acc, slots, counts = rest[2 * HOPS + 4 :]
    own_base = 1 + HOPS * carried
    slot_count = own_base + blocks_here
    scale = 1.0 / math.sqrt(HEAD_WIDTH)
    log2e = math.log2(math.e)
    rows = CHUNK_HEADS * BLOCK_TOKENS

    @pl.when(pl.program_id(0) == 0)
    def _():
        position = lax.axis_index("ctx")
        for qb in range(blocks_here):
            own = position * blocks_here + qb
            slots[qb, 0] = 0

            def climb(step, state):
                current, count = state
                current = parents_ref[current]
                device = lax.div(current, blocks_here)
                slot = lax.rem(current, blocks_here)
                back = position - device
                far = 1 + (HOPS - back) * carried + (slot if carried > 1 else 0)
                where_held = jnp.where(back == 0, own_base + slot, far)
                seen = (current > 0) & (back <= HOPS)

                @pl.when(seen)
                def _():
                    slots[qb, count] = where_held

                return current, count + seen.astype(jnp.int32)

            _, count = lax.fori_loop(
                0, (HOPS + 1) * blocks_here, climb, (own, jnp.int32(1))
            )

            @pl.when(own > 0)
            def _():
                slots[qb, count] = own_base + qb

            counts[qb] = jnp.where(own > 0, count + 1, 1)

    k_all[0] = root_ref[0]
    v_all[0] = root_ref[1]
    for at, piece in enumerate(pieces):
        for e in range(carried):
            k_all[1 + at * carried + e] = piece[0, e * BLOCK_TOKENS : (e + 1) * BLOCK_TOKENS]
            v_all[1 + at * carried + e] = piece[1, e * BLOCK_TOKENS : (e + 1) * BLOCK_TOKENS]
    for b in range(blocks_here):
        k_all[own_base + b] = k_own[b * BLOCK_TOKENS : (b + 1) * BLOCK_TOKENS]
        v_all[own_base + b] = v_own[b * BLOCK_TOKENS : (b + 1) * BLOCK_TOKENS]
    gk_acc[...] = jnp.zeros_like(gk_acc)
    gv_acc[...] = jnp.zeros_like(gv_acc)

    def run_block(qb, seen):
        held = [slots[qb, j] for j in range(seen)]
        tokens = pl.ds(pl.multiple_of(qb * BLOCK_TOKENS, BLOCK_TOKENS), BLOCK_TOKENS)

        def run_chunk(chunk, carry):
            cols = [
                pl.ds(pl.multiple_of((chunk * CHUNK_HEADS + h) * HEAD_WIDTH, HEAD_WIDTH), HEAD_WIDTH)
                for h in range(CHUNK_HEADS)
            ]
            q = jnp.concatenate([q_ref[tokens, c] for c in cols], axis=0)
            do = jnp.concatenate([do_ref[tokens, c] for c in cols], axis=0)
            keys = [k_all[s] for s in held]
            values = [v_all[s] for s in held]
            scores = [dot(q, k, NT) for k in keys]
            token = lax.broadcasted_iota(jnp.int32, (rows, BLOCK_TOKENS), 0) % BLOCK_TOKENS
            other = lax.broadcasted_iota(jnp.int32, (rows, BLOCK_TOKENS), 1)
            scores[-1] = jnp.where(other <= token, scores[-1], -jnp.inf)
            top = functools.reduce(jnp.maximum, scores)
            top = jnp.max(top, axis=1, keepdims=True) * (scale * log2e)
            raised = [jnp.exp2(s * (scale * log2e) - top) for s in scores]
            total = jnp.sum(functools.reduce(jnp.add, raised), axis=1, keepdims=True)
            inverse = 1.0 / total
            probs = [r * inverse for r in raised]
            weights = [p.astype(jnp.bfloat16) for p in probs]
            attended = functools.reduce(
                jnp.add, [dot(w, v, NN) for w, v in zip(weights, values)]
            ).astype(jnp.bfloat16)
            delta = jnp.sum(
                do.astype(jnp.float32) * attended.astype(jnp.float32), axis=1, keepdims=True
            )
            dscores = [
                (p * (dot(do, v, NT) - delta)).astype(jnp.bfloat16) for p, v in zip(probs, values)
            ]
            grad_q = functools.reduce(
                jnp.add, [dot(d, k, NN) for d, k in zip(dscores, keys)]
            )
            grad_q = (grad_q * scale).astype(jnp.bfloat16)
            for h, c in enumerate(cols):
                part = slice(h * BLOCK_TOKENS, (h + 1) * BLOCK_TOKENS)
                out_ref[tokens, c] = attended[part]
                gq_ref[tokens, c] = grad_q[part]
            for s, d, w in zip(held, dscores, weights):
                gk_acc[s] += dot(q, d, TN)
                gv_acc[s] += dot(do, w, TN)
            return carry

        lax.fori_loop(0, heads_per_group // CHUNK_HEADS, run_chunk, 0)

    @pl.loop(0, blocks_here)
    def _(qb):
        seen_here = counts[qb]
        for seen in range(1, slot_count + 1):
            pl.when(seen_here == seen)(functools.partial(run_block, qb, seen))

    def grads(slot):
        return (gk_acc[slot] * scale).T, gv_acc[slot].T

    for b in range(blocks_here):
        part = slice(b * BLOCK_TOKENS, (b + 1) * BLOCK_TOKENS)
        gown_ref[0, part], gown_ref[1, part] = grads(own_base + b)
    groot_ref[0], groot_ref[1] = grads(0)
    for at, piece in enumerate(gpieces):
        for e in range(carried):
            part = slice(e * BLOCK_TOKENS, (e + 1) * BLOCK_TOKENS)
            gk, gv = grads(1 + at * carried + e)
            piece[0, part] = gk.astype(jnp.bfloat16)
            piece[1, part] = gv.astype(jnp.bfloat16)


def attention(carried, parents, query, grad, key, value, root_pair, pieces):
    tokens_here = query.shape[0]
    blocks_here = tokens_here // BLOCK_TOKENS
    groups = key.shape[1] // HEAD_WIDTH
    heads_per_group = query.shape[1] // HEAD_WIDTH // groups
    wide = pl.BlockSpec((tokens_here, heads_per_group * HEAD_WIDTH), lambda g, _: (0, g))
    narrow = pl.BlockSpec((tokens_here, HEAD_WIDTH), lambda g, _: (0, g))
    pair = lambda count: pl.BlockSpec((2, count, HEAD_WIDTH), lambda g, _: (0, 0, g))
    root_spec = pair(BLOCK_TOKENS)
    piece_spec = pair(carried * BLOCK_TOKENS)
    own_spec = pair(tokens_here)
    slot_count = 1 + HOPS * carried + blocks_here
    pair_shape = lambda like, kind: jax.ShapeDtypeStruct(like.shape, kind)
    blocks = pltpu.VMEM((slot_count, BLOCK_TOKENS, HEAD_WIDTH), jnp.bfloat16)
    sums = pltpu.VMEM((slot_count, HEAD_WIDTH, BLOCK_TOKENS), jnp.float32)
    return pl.pallas_call(
        functools.partial(attention_kernel, carried, blocks_here, heads_per_group),
        grid_spec=pltpu.PrefetchScalarGridSpec(
            num_scalar_prefetch=1,
            grid=(groups,),
            in_specs=[wide, wide, narrow, narrow, root_spec] + [piece_spec] * HOPS,
            out_specs=[wide, wide, own_spec, root_spec] + [piece_spec] * HOPS,
            scratch_shapes=[
                blocks,
                blocks,
                sums,
                sums,
                pltpu.SMEM((blocks_here, slot_count), jnp.int32),
                pltpu.SMEM((blocks_here,), jnp.int32),
            ],
        ),
        out_shape=[
            pair_shape(query, jnp.bfloat16),
            pair_shape(query, jnp.bfloat16),
            jax.ShapeDtypeStruct((2,) + key.shape, jnp.float32),
            pair_shape(root_pair, jnp.float32),
        ]
        + [pair_shape(p, jnp.bfloat16) for p in pieces],
        compiler_params=pltpu.CompilerParams(vmem_limit_bytes=48 << 20),
        name=f"tree_attention_{carried}",
    )(parents, query, grad, key, value, root_pair, *pieces)


def run(carried, choice, query, key, value, output_cotangent, parents):
    tokens_here = query.shape[0]
    blocks_here = tokens_here // BLOCK_TOKENS
    position = lax.axis_index("ctx")
    key_value = jnp.stack([key, value])
    root_pair = spread_from_first(key_value[:, :BLOCK_TOKENS])
    if carried == blocks_here:
        sent = key_value
    else:
        mine = choice[position]
        sent = lax.dynamic_slice_in_dim(key_value, mine * BLOCK_TOKENS, BLOCK_TOKENS, 1)
    pieces = [passed_along(sent, back) for back in range(HOPS, 0, -1)]
    out, grad_q, own, root_terms, *terms = attention(
        carried, parents, query, output_cotangent, key, value, root_pair, pieces
    )
    returned = sum(
        passed_along(terms[HOPS - back], -back).astype(jnp.float32)
        for back in range(1, HOPS + 1)
    )
    root_sum = sum_to_first(root_terms)
    root_rows = jnp.where(position == 0, root_sum, 0.0)
    parts = []
    for b in range(blocks_here):
        rows = slice(b * BLOCK_TOKENS, (b + 1) * BLOCK_TOKENS)
        part = own[:, rows]
        if carried == blocks_here:
            part = part + returned[:, rows]
        else:
            part = part + jnp.where(mine == b, returned, 0.0)
        if b == 0:
            part = part + root_rows
        parts.append(part)
    total = jnp.concatenate(parts, axis=1).astype(jnp.bfloat16)
    return out, grad_q, total[0], total[1]


def local(query, key, value, output_cotangent, parents):
    blocks_here = query.shape[0] // BLOCK_TOKENS
    choice = exported_blocks(parents, blocks_here)
    operands = (choice, query, key, value, output_cotangent, parents)
    return lax.cond(
        choice[-1] > 1,
        functools.partial(run, blocks_here),
        functools.partial(run, 1),
        *operands,
    )


def solution(mesh):
    in_specs = (P("ctx", "tp"), P("ctx", "tp"), P("ctx", "tp"), P("ctx", "tp"), P())
    out_specs = (P("ctx", "tp"), P("ctx", "tp"), P("ctx", "tp"), P("ctx", "tp"))
    return jax.shard_map(local, mesh=mesh, in_specs=in_specs, out_specs=out_specs, check_vma=False)
```

```python
import functools
import math

import jax
import jax.numpy as jnp
from jax import lax
from jax.experimental import pallas as pl
from jax.experimental.pallas import tpu as pltpu
from jax.sharding import PartitionSpec as P

HEAD_WIDTH = 128
BLOCK_TOKENS = 128
HOPS = 3
LAYER = 4


def passed_along(array, by):
    devices = lax.axis_size("ctx")
    pairs = [(i, i + by) for i in range(devices) if 0 <= i + by < devices]
    return lax.ppermute(array, "ctx", pairs)


def layer_stages(layers):
    stages = []
    while layers > 1:
        fan = 4 if layers % 4 == 0 else (2 if layers % 2 == 0 else layers)
        layers //= fan
        stages.append((layers, fan))
    return stages


def spread_from_first(held, after=()):
    devices = lax.axis_size("ctx")
    position = lax.axis_index("ctx")
    layers = devices // LAYER
    layer = position // LAYER
    for stride, fan in layer_stages(layers):
        bases = range(0, layers, stride * fan)
        arrived = [
            lax.ppermute(held, "ctx", [(b * LAYER, (b + j * stride) * LAYER) for b in bases])
            for j in range(1, fan)
        ]
        held, *arrived = lax.optimization_barrier((held, *arrived))
        for j, piece in enumerate(arrived, 1):
            here = (position % LAYER == 0) & (layer % (stride * fan) == j * stride)
            held = jnp.where(here, piece, held)
    held, *after = lax.optimization_barrier((held, *after))
    for step in (2, 1):
        pairs = [(i, i + step) for i in range(0, devices, 2 * step)]
        here = (position % (2 * step)) == step
        held = jnp.where(here, lax.ppermute(held, "ctx", pairs), held)
    return (held, *after)


def sum_to_first(total, after=()):
    devices = lax.axis_size("ctx")
    layers = devices // LAYER
    home = lambda layer: layer * LAYER + (2 if layer else 0)
    stages = [[[(i + 1, i) for i in range(0, devices, 2)]]]
    stages.append([[(home(l) ^ 2, home(l)) for l in range(layers)]])
    for stride, fan in reversed(layer_stages(layers)):
        bases = range(0, layers, stride * fan)
        stages.append(
            [[(home(b + j * stride), home(b)) for b in bases] for j in range(1, fan)]
        )
    for at, stage in enumerate(stages):
        sent = total.astype(jnp.bfloat16)
        arrived = [lax.ppermute(sent, "ctx", pairs) for pairs in stage]
        if at == 0:
            arrived[0], *after = lax.optimization_barrier((arrived[0], *after))
        for piece in arrived:
            total = total + piece.astype(jnp.float32)
    return (total, *after)


def export_kernel(
    blocks_here, parents_ref, k_ref, v_ref, choice_ref, crowded_ref, first_ref, sent_ref, reach_ref
):
    block_count = parents_ref.shape[0]
    for b in range(block_count):
        reach_ref[b] = jnp.int32(b // blocks_here)
    crowded = jnp.int32(0)
    for device in reversed(range(block_count // blocks_here)):
        count = jnp.int32(0)
        choice = jnp.int32(0)
        for slot in reversed(range(blocks_here)):
            block = device * blocks_here + slot
            if block == 0:
                continue
            last = reach_ref[block]
            up = parents_ref[block]
            reach_ref[up] = jnp.maximum(reach_ref[up], last)
            read = last > device
            count = count + read.astype(jnp.int32)
            choice = jnp.where(read, slot, choice)
        choice_ref[device] = choice
        crowded = jnp.maximum(crowded, count)
    crowded_ref[0] = crowded
    mine = choice_ref[lax.axis_index("ctx")]
    rows = pl.ds(pl.multiple_of(mine * BLOCK_TOKENS, BLOCK_TOKENS), BLOCK_TOKENS)
    for which, ref in enumerate((k_ref, v_ref)):
        first_ref[which] = ref[:BLOCK_TOKENS]
        sent_ref[which] = ref[rows]


def exported_blocks(parents, key, value):
    blocks_here = key.shape[0] // BLOCK_TOKENS
    block_count = parents.shape[0]
    smem = pl.BlockSpec(memory_space=pltpu.SMEM)
    vmem = pl.BlockSpec(memory_space=pltpu.VMEM)
    pair = jax.ShapeDtypeStruct((2, BLOCK_TOKENS, key.shape[1]), key.dtype)
    return pl.pallas_call(
        functools.partial(export_kernel, blocks_here),
        out_shape=[
            jax.ShapeDtypeStruct((block_count // blocks_here,), jnp.int32),
            jax.ShapeDtypeStruct((1,), jnp.int32),
            pair,
            pair,
        ],
        in_specs=[smem, vmem, vmem],
        out_specs=[smem, smem, vmem, vmem],
        scratch_shapes=[pltpu.SMEM((block_count,), jnp.int32)],
        name="exported",
    )(parents, key, value)


NT = (((1,), (1,)), ((), ()))
NN = (((1,), (0,)), ((), ()))
TN = (((0,), (0,)), ((), ()))


def dot(a, b, dims):
    return lax.dot_general(a, b, dims, preferred_element_type=jnp.float32)


def attention_kernel(
    plan, blocks_here, heads_per_group, parents_ref, q_ref, do_ref, k_own, v_own, root_ref, *rest
):
    held_counts, slot_of, chunk_heads, sub_heads, skew = plan
    arrivals = rest[: len(held_counts)]
    (out_ref, gq_ref, gown_ref, groot_ref) = rest[len(held_counts) : len(held_counts) + 4]
    departures = rest[len(held_counts) + 4 : 2 * len(held_counts) + 4]
    k_all, v_all, gk_acc, gv_acc, slots, counts = rest[2 * len(held_counts) + 4 :]
    own_base = 1 + sum(held_counts)
    scale = 1.0 / math.sqrt(HEAD_WIDTH)
    log2e = math.log2(math.e)
    rows = sub_heads * BLOCK_TOKENS
    most_seen = slots.shape[1]

    @pl.when(pl.program_id(0) == 0)
    def _():
        position = lax.axis_index("ctx")
        for qb in range(blocks_here):
            own = position * blocks_here + qb
            slots[qb, 0] = 0

            def climb(step, state):
                current, count = state
                current = parents_ref[current]
                device = lax.div(current, blocks_here)
                slot = lax.rem(current, blocks_here)
                back = position - device
                where_held = jnp.where(back == 0, own_base + slot, slot_of(position, back, slot))
                seen = (current > 0) & (back <= HOPS)

                @pl.when(seen)
                def _():
                    slots[qb, count] = where_held

                return current, count + seen.astype(jnp.int32)

            _, count = lax.fori_loop(
                0, (HOPS + 1) * blocks_here, climb, (own, jnp.int32(1))
            )

            @pl.when(own > 0)
            def _():
                slots[qb, count] = own_base + qb

            counts[qb] = jnp.where(own > 0, count + 1, 1)

    k_all[0] = root_ref[0]
    v_all[0] = root_ref[1]
    at = 1
    for arrival, count in zip(arrivals, held_counts):
        for e in range(count):
            part = slice(e * BLOCK_TOKENS, (e + 1) * BLOCK_TOKENS)
            k_all[at] = arrival[0, part]
            v_all[at] = arrival[1, part]
            at += 1
    for b in range(blocks_here):
        k_all[own_base + b] = k_own[b * BLOCK_TOKENS : (b + 1) * BLOCK_TOKENS]
        v_all[own_base + b] = v_own[b * BLOCK_TOKENS : (b + 1) * BLOCK_TOKENS]
    gk_acc[...] = jnp.zeros_like(gk_acc)
    gv_acc[...] = jnp.zeros_like(gv_acc)

    def run_block(qb, seen):
        held = [slots[qb, j] for j in range(seen)]
        tokens = pl.ds(pl.multiple_of(qb * BLOCK_TOKENS, BLOCK_TOKENS), BLOCK_TOKENS)

        keys = jnp.concatenate([k_all[s] for s in held], axis=0)
        values = jnp.concatenate([v_all[s] for s in held], axis=0)
        split = lambda wide: [
            wide[:, j * BLOCK_TOKENS : (j + 1) * BLOCK_TOKENS] for j in range(seen)
        ]

        def run_chunk(chunk, carry):
            def load(ref, sub):
                return jnp.concatenate([ref[tokens, c] for c in columns(sub)], axis=0)

            def columns(sub):
                return [
                    pl.ds(
                        pl.multiple_of((chunk * chunk_heads + sub * sub_heads + h) * HEAD_WIDTH, HEAD_WIDTH),
                        HEAD_WIDTH,
                    )
                    for h in range(sub_heads)
                ]

            def first(sub):
                q, do = load(q_ref, sub), load(do_ref, sub)
                return dot(q, keys, NT), dot(do, values, NT)

            def second(sub, scores, gprobs):
                scores = split(scores)
                token = lax.broadcasted_iota(jnp.int32, (rows, BLOCK_TOKENS), 0) % BLOCK_TOKENS
                other = lax.broadcasted_iota(jnp.int32, (rows, BLOCK_TOKENS), 1)
                scores[-1] = jnp.where(other <= token, scores[-1], -jnp.inf)
                top = functools.reduce(jnp.maximum, scores)
                top = jnp.max(top, axis=1, keepdims=True) * (scale * log2e)
                raised = [jnp.exp2(s * (scale * log2e) - top) for s in scores]
                total = jnp.sum(functools.reduce(jnp.add, raised), axis=1, keepdims=True)
                inverse = 1.0 / total
                probs = [r * inverse for r in raised]
                weights = jnp.concatenate([p.astype(jnp.bfloat16) for p in probs], axis=1)
                attended = dot(weights, values, NN).astype(jnp.bfloat16)
                for h, c in enumerate(columns(sub)):
                    out_ref[tokens, c] = attended[h * BLOCK_TOKENS : (h + 1) * BLOCK_TOKENS]
                return probs, weights, attended, gprobs

            def third(sub, probs, weights, attended, gprobs):
                q, do = load(q_ref, sub), load(do_ref, sub)
                delta = jnp.sum(
                    do.astype(jnp.float32) * attended.astype(jnp.float32), axis=1, keepdims=True
                )
                dscores = jnp.concatenate(
                    [(p * (g - delta)).astype(jnp.bfloat16) for p, g in zip(probs, split(gprobs))],
                    axis=1,
                )
                grad_q = (dot(dscores, keys, NN) * scale).astype(jnp.bfloat16)
                for h, c in enumerate(columns(sub)):
                    gq_ref[tokens, c] = grad_q[h * BLOCK_TOKENS : (h + 1) * BLOCK_TOKENS]
                gk = split(dot(q, dscores, TN))
                gv = split(dot(do, weights, TN))
                for s, x, y in zip(held, gk, gv):
                    gk_acc[s] += x
                    gv_acc[s] += y

            subs = chunk_heads // sub_heads
            one, two = {}, {}
            for turn in range(subs + 2 * skew):
                if turn < subs:
                    one[turn] = first(turn)
                if 0 <= turn - skew < subs:
                    two[turn - skew] = second(turn - skew, *one.pop(turn - skew))
                if 0 <= turn - 2 * skew < subs:
                    third(turn - 2 * skew, *two.pop(turn - 2 * skew))
            return carry

        lax.fori_loop(0, heads_per_group // chunk_heads, run_chunk, 0)

    @pl.loop(0, blocks_here)
    def _(qb):
        seen_here = counts[qb]
        for seen in range(1, most_seen + 1):
            pl.when(seen_here == seen)(functools.partial(run_block, qb, seen))

    def grads(slot):
        return (gk_acc[slot] * scale).T, gv_acc[slot].T

    for b in range(blocks_here):
        part = slice(b * BLOCK_TOKENS, (b + 1) * BLOCK_TOKENS)
        gown_ref[0, part], gown_ref[1, part] = grads(own_base + b)
    groot_ref[0], groot_ref[1] = grads(0)
    at = 1
    for departure, count in zip(departures, held_counts):
        for e in range(count):
            part = slice(e * BLOCK_TOKENS, (e + 1) * BLOCK_TOKENS)
            gk, gv = grads(at)
            departure[0, part] = gk.astype(jnp.bfloat16)
            departure[1, part] = gv.astype(jnp.bfloat16)
            at += 1


def attention(plan, most_seen, parents, query, grad, key, value, root_pair, arrivals):
    tokens_here = query.shape[0]
    blocks_here = tokens_here // BLOCK_TOKENS
    groups = key.shape[1] // HEAD_WIDTH
    heads_per_group = query.shape[1] // HEAD_WIDTH // groups
    wide = pl.BlockSpec((tokens_here, heads_per_group * HEAD_WIDTH), lambda g, _: (0, g))
    narrow = pl.BlockSpec((tokens_here, HEAD_WIDTH), lambda g, _: (0, g))
    pair = lambda rows: pl.BlockSpec((2, rows, HEAD_WIDTH), lambda g, _: (0, 0, g))
    arrival_specs = [pair(a.shape[1]) for a in arrivals]
    slot_count = 1 + sum(plan[0]) + blocks_here
    like = lambda array, kind: jax.ShapeDtypeStruct(array.shape, kind)
    blocks = pltpu.VMEM((slot_count, BLOCK_TOKENS, HEAD_WIDTH), jnp.bfloat16)
    sums = pltpu.VMEM((slot_count, HEAD_WIDTH, BLOCK_TOKENS), jnp.float32)
    return pl.pallas_call(
        functools.partial(attention_kernel, plan, blocks_here, heads_per_group),
        grid_spec=pltpu.PrefetchScalarGridSpec(
            num_scalar_prefetch=1,
            grid=(groups,),
            in_specs=[wide, wide, narrow, narrow, pair(BLOCK_TOKENS)] + arrival_specs,
            out_specs=[wide, wide, pair(tokens_here), pair(BLOCK_TOKENS)] + arrival_specs,
            scratch_shapes=[
                blocks,
                blocks,
                sums,
                sums,
                pltpu.SMEM((blocks_here, most_seen), jnp.int32),
                pltpu.SMEM((blocks_here,), jnp.int32),
            ],
        ),
        out_shape=[
            like(query, jnp.bfloat16),
            like(query, jnp.bfloat16),
            jax.ShapeDtypeStruct((2,) + key.shape, jnp.float32),
            like(root_pair, jnp.float32),
        ]
        + [like(a, jnp.bfloat16) for a in arrivals],
        compiler_params=pltpu.CompilerParams(vmem_limit_bytes=48 << 20),
        name=f"tree_attention_{most_seen}",
    )(parents, query, grad, key, value, root_pair, *arrivals)


def wide32(array):
    return array.astype(jnp.float32)


def run_every_block(choice, first, sent, query, key, value, output_cotangent, parents):
    blocks_here = query.shape[0] // BLOCK_TOKENS
    position = lax.axis_index("ctx")
    key_value = jnp.stack([key, value])
    (root_pair,) = spread_from_first(first)
    pieces = [passed_along(key_value, back) for back in range(HOPS, 0, -1)]
    slot_of = lambda position, back, slot: 1 + (HOPS - back) * blocks_here + slot
    plan = ((blocks_here,) * HOPS, slot_of, 2, 2, 0)
    out, grad_q, own, root_terms, *terms = attention(
        plan, 1 + (HOPS + 1) * blocks_here, parents, query, output_cotangent, key, value,
        root_pair, pieces,
    )
    total = own + sum(
        wide32(passed_along(terms[HOPS - back], -back)) for back in range(1, HOPS + 1)
    )
    root_rows = jnp.where(position == 0, sum_to_first(root_terms)[0], 0.0)
    total = jnp.concatenate(
        [total[:, :BLOCK_TOKENS] + root_rows, total[:, BLOCK_TOKENS:]], axis=1
    ).astype(jnp.bfloat16)
    return out, grad_q, total[0], total[1]


def run_one_block(choice, first, sent, query, key, value, output_cotangent, parents):
    blocks_here = query.shape[0] // BLOCK_TOKENS
    devices = lax.axis_size("ctx")
    position = lax.axis_index("ctx")
    odd = position % 2
    swap = [(i, i ^ 1) for i in range(devices)]
    skip = [(i, i + 3) for i in range(1, devices - 3, 2)]
    mine = choice[position]
    two_back = passed_along(sent, 2)
    three_back = lax.ppermute(sent, "ctx", skip)
    root_pair, two_back, three_back = spread_from_first(first, (two_back, three_back))
    across = lax.ppermute(jnp.concatenate([two_back, sent], axis=1), "ctx", swap)

    def slot_of(position, back, slot):
        odd = lax.rem(position, 2)
        return jnp.where(back == 2, 2, jnp.where(back == 1, 3 + odd, 1 + 2 * odd))

    plan = ((1, 1, 2), slot_of, 8, 2, 1)
    out, grad_q, own, root_terms, g_three, g_two, g_across = attention(
        plan, 1 + HOPS + blocks_here, parents, query, output_cotangent, key, value, root_pair,
        [three_back, two_back, across],
    )
    from_core = lax.ppermute(g_across, "ctx", swap)
    from_three = lax.ppermute(g_three, "ctx", [(b, a) for a, b in skip])
    root_sum, from_core = sum_to_first(root_terms, (from_core,))
    merged = wide32(g_two) + wide32(from_core[:, :BLOCK_TOKENS])
    from_two = passed_along(merged.astype(jnp.bfloat16), -2)

    block = lax.broadcasted_iota(jnp.int32, (blocks_here, BLOCK_TOKENS, key.shape[1]), 0)
    at_first = (block == 0) & (position == 0)

    def final(which):
        returned = (
            wide32(from_two[which]) + wide32(from_three[which])
            + jnp.where(odd == 0, wide32(from_core[which, BLOCK_TOKENS:]), 0.0)
        )
        total = own[which].reshape(block.shape)
        total = total + jnp.where(block == mine, returned[None], 0.0)
        total = total + jnp.where(at_first, root_sum[which][None], 0.0)
        return total.astype(jnp.bfloat16).reshape(key.shape)

    return out, grad_q, final(0), final(1)


def local(query, key, value, output_cotangent, parents):
    choice, crowded, first, sent = exported_blocks(parents, key, value)
    return lax.cond(
        crowded[0] > 1,
        run_every_block,
        run_one_block,
        choice, first, sent, query, key, value, output_cotangent, parents,
    )


def solution(mesh):
    in_specs = (P("ctx", "tp"), P("ctx", "tp"), P("ctx", "tp"), P("ctx", "tp"), P())
    out_specs = (P("ctx", "tp"), P("ctx", "tp"), P("ctx", "tp"), P("ctx", "tp"))
    return jax.shard_map(local, mesh=mesh, in_specs=in_specs, out_specs=out_specs, check_vma=False)
```

```python
import functools
import math

import jax
import jax.numpy as jnp
from jax import lax
from jax.experimental import pallas as pl
from jax.experimental.pallas import tpu as pltpu
from jax.sharding import PartitionSpec as P

HEAD_WIDTH = 128
BLOCK_TOKENS = 128
HOPS = 3
LAYER = 4
SUB_HEADS = 2
SPAN = 2
QUICK = (2, 3, 4, 5)


def passed_along(array, by):
    devices = lax.axis_size("ctx")
    pairs = [(i, i + by) for i in range(devices) if 0 <= i + by < devices]
    return lax.ppermute(array, "ctx", pairs)


def layer_stages(layers):
    stages = []
    while layers > 1:
        fan = 4 if layers % 4 == 0 else (2 if layers % 2 == 0 else layers)
        layers //= fan
        stages.append((layers, fan))
    return stages


def spread_from_first(held, after=()):
    devices = lax.axis_size("ctx")
    position = lax.axis_index("ctx")
    layers = devices // LAYER
    layer = position // LAYER
    for stride, fan in layer_stages(layers):
        bases = range(0, layers, stride * fan)
        arrived = [
            lax.ppermute(held, "ctx", [(b * LAYER, (b + j * stride) * LAYER) for b in bases])
            for j in range(1, fan)
        ]
        held, *arrived = lax.optimization_barrier((held, *arrived))
        for j, piece in enumerate(arrived, 1):
            here = (position % LAYER == 0) & (layer % (stride * fan) == j * stride)
            held = jnp.where(here, piece, held)
    held, *after = lax.optimization_barrier((held, *after))
    for step in (2, 1):
        pairs = [(i, i + step) for i in range(0, devices, 2 * step)]
        here = (position % (2 * step)) == step
        held = jnp.where(here, lax.ppermute(held, "ctx", pairs), held)
    return (held, *after)


def sum_to_first(total, after=()):
    devices = lax.axis_size("ctx")
    layers = devices // LAYER
    home = lambda layer: layer * LAYER + (2 if layer else 0)
    stages = [[[(i + 1, i) for i in range(0, devices, 2)]]]
    stages.append([[(home(l) ^ 2, home(l)) for l in range(layers)]])
    for stride, fan in reversed(layer_stages(layers)):
        bases = range(0, layers, stride * fan)
        stages.append(
            [[(home(b + j * stride), home(b)) for b in bases] for j in range(1, fan)]
        )
    for at, stage in enumerate(stages):
        sent = total.astype(jnp.bfloat16)
        arrived = [lax.ppermute(sent, "ctx", pairs) for pairs in stage]
        if at == 1:
            arrived[0], *after = lax.optimization_barrier((arrived[0], *after))
        for piece in arrived:
            total = total + piece.astype(jnp.float32)
    return (total, *after)


def export_kernel(
    blocks_here, parents_ref, k_ref, v_ref, choice_ref, crowded_ref, first_ref, sent_ref,
    reach_ref, choices_ref
):
    block_count = parents_ref.shape[0]
    for b in range(block_count):
        reach_ref[b] = jnp.int32(b // blocks_here)
    crowded = jnp.int32(0)
    for device in reversed(range(block_count // blocks_here)):
        count = jnp.int32(0)
        choice = jnp.int32(0)
        for slot in reversed(range(blocks_here)):
            block = device * blocks_here + slot
            if block == 0:
                continue
            last = reach_ref[block]
            up = parents_ref[block]
            reach_ref[up] = jnp.maximum(reach_ref[up], last)
            read = last > device
            count = count + read.astype(jnp.int32)
            choice = jnp.where(read, slot, choice)
        choices_ref[device] = choice
        crowded = jnp.maximum(crowded, count)
    crowded_ref[0] = crowded
    mine = choices_ref[lax.axis_index("ctx")]
    choice_ref[0] = mine
    rows = pl.ds(pl.multiple_of(mine * BLOCK_TOKENS, BLOCK_TOKENS), BLOCK_TOKENS)
    for which, ref in enumerate((k_ref, v_ref)):
        first_ref[which] = ref[:BLOCK_TOKENS]
        sent_ref[which] = ref[rows]


def exported_blocks(parents, key, value):
    blocks_here = key.shape[0] // BLOCK_TOKENS
    block_count = parents.shape[0]
    smem = pl.BlockSpec(memory_space=pltpu.SMEM)
    vmem = pl.BlockSpec(memory_space=pltpu.VMEM)
    pair = jax.ShapeDtypeStruct((2, BLOCK_TOKENS, key.shape[1]), key.dtype)
    return pl.pallas_call(
        functools.partial(export_kernel, blocks_here),
        out_shape=[
            jax.ShapeDtypeStruct((1,), jnp.int32),
            jax.ShapeDtypeStruct((1,), jnp.int32),
            pair,
            pair,
        ],
        in_specs=[smem, vmem, vmem],
        out_specs=[smem, smem, vmem, vmem],
        scratch_shapes=[
            pltpu.SMEM((block_count,), jnp.int32),
            pltpu.SMEM((block_count // blocks_here,), jnp.int32),
        ],
        name="exported",
    )(parents, key, value)


NT = (((1,), (1,)), ((), ()))
NN = (((1,), (0,)), ((), ()))
TN = (((0,), (0,)), ((), ()))


def dot(a, b, dims):
    return lax.dot_general(a, b, dims, preferred_element_type=jnp.float32)


def attention_kernel(
    plan, blocks_here, heads_per_group, span, parents_ref, q_ref, do_ref, k_own, v_own, root_ref, *rest
):
    held_counts, slot_of, quick_counts = plan
    arrivals = rest[: len(held_counts)]
    (out_ref, gq_ref, gown_ref, groot_ref) = rest[len(held_counts) : len(held_counts) + 4]
    departures = rest[len(held_counts) + 4 : 2 * len(held_counts) + 4]
    k_all, v_all, gk_acc, gv_acc, slots, counts = rest[2 * len(held_counts) + 4 :]
    own_base = 1 + sum(held_counts)
    scale = 1.0 / math.sqrt(HEAD_WIDTH)
    log2e = math.log2(math.e)
    rows = SUB_HEADS * BLOCK_TOKENS
    groups = [slice(g * HEAD_WIDTH, (g + 1) * HEAD_WIDTH) for g in range(span)]
    most_seen = slots.shape[1]

    @pl.when(pl.program_id(0) == 0)
    def _():
        position = lax.axis_index("ctx")
        for qb in range(blocks_here):
            own = position * blocks_here + qb
            slots[qb, 0] = 0

            def climb(step, state):
                current, count = state
                current = parents_ref[current]
                device = lax.div(current, blocks_here)
                slot = lax.rem(current, blocks_here)
                back = position - device
                where_held = jnp.where(back == 0, own_base + slot, slot_of(position, back, slot))
                seen = (current > 0) & (back <= HOPS)

                @pl.when(seen)
                def _():
                    slots[qb, count] = where_held

                return current, count + seen.astype(jnp.int32)

            _, count = lax.fori_loop(
                0, (HOPS + 1) * blocks_here, climb, (own, jnp.int32(1))
            )

            @pl.when(own > 0)
            def _():
                slots[qb, count] = own_base + qb

            counts[qb] = jnp.where(own > 0, count + 1, 1)

    for g, cols in enumerate(groups):
        k_all[g, 0] = root_ref[0, :, cols]
        v_all[g, 0] = root_ref[1, :, cols]
        at = 1
        for arrival, count in zip(arrivals, held_counts):
            for e in range(count):
                part = slice(e * BLOCK_TOKENS, (e + 1) * BLOCK_TOKENS)
                k_all[g, at] = arrival[0, part, cols]
                v_all[g, at] = arrival[1, part, cols]
                at += 1
        for b in range(blocks_here):
            part = slice(b * BLOCK_TOKENS, (b + 1) * BLOCK_TOKENS)
            k_all[g, own_base + b] = k_own[part, cols]
            v_all[g, own_base + b] = v_own[part, cols]
    gk_acc[...] = jnp.zeros_like(gk_acc)
    gv_acc[...] = jnp.zeros_like(gv_acc)

    def run_block(qb, seen):
        held = [slots[qb, j] for j in range(seen)]
        tokens = pl.ds(pl.multiple_of(qb * BLOCK_TOKENS, BLOCK_TOKENS), BLOCK_TOKENS)
        quick = seen in quick_counts
        chunk_heads = span * heads_per_group if quick else SUB_HEADS
        skew = 1 if quick else 0
        split = lambda wide: [
            wide[:, j * BLOCK_TOKENS : (j + 1) * BLOCK_TOKENS] for j in range(seen)
        ]

        def run_chunk(chunk):
            def load(ref, sub):
                return jnp.concatenate([ref[tokens, c] for c in columns(sub)], axis=0)

            def columns(sub):
                heads = [chunk * chunk_heads + sub * SUB_HEADS + h for h in range(SUB_HEADS)]
                return [pl.ds(pl.multiple_of(h * HEAD_WIDTH, HEAD_WIDTH), HEAD_WIDTH) for h in heads]

            def group_of(sub):
                return (chunk * chunk_heads + sub * SUB_HEADS) // heads_per_group

            def blocks(ref, sub):
                return jnp.concatenate([ref[group_of(sub), s] for s in held], axis=0)

            def first(sub):
                q, do = load(q_ref, sub), load(do_ref, sub)
                return dot(q, blocks(k_all, sub), NT), dot(do, blocks(v_all, sub), NT)

            def second(sub, scores, gprobs):
                scores = split(scores)
                token = lax.broadcasted_iota(jnp.int32, (rows, BLOCK_TOKENS), 0) % BLOCK_TOKENS
                other = lax.broadcasted_iota(jnp.int32, (rows, BLOCK_TOKENS), 1)
                scores[-1] = jnp.where(other <= token, scores[-1], -jnp.inf)
                top = functools.reduce(jnp.maximum, scores)
                top = jnp.max(top, axis=1, keepdims=True) * (scale * log2e)
                raised = [jnp.exp2(s * (scale * log2e) - top) for s in scores]
                total = jnp.sum(functools.reduce(jnp.add, raised), axis=1, keepdims=True)
                inverse = 1.0 / total
                probs = [r * inverse for r in raised]
                weights = jnp.concatenate([p.astype(jnp.bfloat16) for p in probs], axis=1)
                attended = dot(weights, blocks(v_all, sub), NN).astype(jnp.bfloat16)
                for h, c in enumerate(columns(sub)):
                    out_ref[tokens, c] = attended[h * BLOCK_TOKENS : (h + 1) * BLOCK_TOKENS]
                return probs, weights, attended, gprobs

            def third(sub, probs, weights, attended, gprobs):
                q, do = load(q_ref, sub), load(do_ref, sub)
                delta = jnp.sum(
                    do.astype(jnp.float32) * attended.astype(jnp.float32), axis=1, keepdims=True
                )
                dscores = jnp.concatenate(
                    [(p * (g - delta)).astype(jnp.bfloat16) for p, g in zip(probs, split(gprobs))],
                    axis=1,
                )
                grad_q = (dot(dscores, blocks(k_all, sub), NN) * scale).astype(jnp.bfloat16)
                for h, c in enumerate(columns(sub)):
                    gq_ref[tokens, c] = grad_q[h * BLOCK_TOKENS : (h + 1) * BLOCK_TOKENS]
                gk = split(dot(q, dscores, TN))
                gv = split(dot(do, weights, TN))
                for s, x, y in zip(held, gk, gv):
                    gk_acc[group_of(sub), s] += x
                    gv_acc[group_of(sub), s] += y

            subs = chunk_heads // SUB_HEADS
            one, two = {}, {}
            for turn in range(subs + 2 * skew):
                if turn < subs:
                    one[turn] = first(turn)
                if 0 <= turn - skew < subs:
                    two[turn - skew] = second(turn - skew, *one.pop(turn - skew))
                if 0 <= turn - 2 * skew < subs:
                    third(turn - 2 * skew, *two.pop(turn - 2 * skew))

        if quick:
            run_chunk(0)
        else:
            pl.loop(0, span * heads_per_group // SUB_HEADS)(run_chunk)

    @pl.loop(0, blocks_here)
    def _(qb):
        seen_here = counts[qb]
        for seen in range(1, most_seen + 1):
            pl.when(seen_here == seen)(functools.partial(run_block, qb, seen))

    for g, cols in enumerate(groups):

        def grads(slot):
            return (gk_acc[g, slot] * scale).T, gv_acc[g, slot].T

        for b in range(blocks_here):
            part = slice(b * BLOCK_TOKENS, (b + 1) * BLOCK_TOKENS)
            gown_ref[0, part, cols], gown_ref[1, part, cols] = grads(own_base + b)
        groot_ref[0, :, cols], groot_ref[1, :, cols] = grads(0)
        at = 1
        for departure, count in zip(departures, held_counts):
            for e in range(count):
                part = slice(e * BLOCK_TOKENS, (e + 1) * BLOCK_TOKENS)
                gk, gv = grads(at)
                departure[0, part, cols] = gk.astype(jnp.bfloat16)
                departure[1, part, cols] = gv.astype(jnp.bfloat16)
                at += 1


def attention(plan, most_seen, parents, query, grad, key, value, root_pair, arrivals):
    tokens_here = query.shape[0]
    blocks_here = tokens_here // BLOCK_TOKENS
    groups = key.shape[1] // HEAD_WIDTH
    heads_per_group = query.shape[1] // HEAD_WIDTH // groups
    span = SPAN if groups % SPAN == 0 else 1
    width = span * HEAD_WIDTH
    wide = pl.BlockSpec((tokens_here, heads_per_group * width), lambda g, _: (0, g))
    narrow = pl.BlockSpec((tokens_here, width), lambda g, _: (0, g))
    pair = lambda rows: pl.BlockSpec((2, rows, width), lambda g, _: (0, 0, g))
    arrival_specs = [pair(a.shape[1]) for a in arrivals]
    slot_count = 1 + sum(plan[0]) + blocks_here
    like = lambda array, kind: jax.ShapeDtypeStruct(array.shape, kind)
    blocks = pltpu.VMEM((span, slot_count, BLOCK_TOKENS, HEAD_WIDTH), jnp.bfloat16)
    sums = pltpu.VMEM((span, slot_count, HEAD_WIDTH, BLOCK_TOKENS), jnp.float32)
    return pl.pallas_call(
        functools.partial(attention_kernel, plan, blocks_here, heads_per_group, span),
        grid_spec=pltpu.PrefetchScalarGridSpec(
            num_scalar_prefetch=1,
            grid=(groups // span,),
            in_specs=[wide, wide, narrow, narrow, pair(BLOCK_TOKENS)] + arrival_specs,
            out_specs=[wide, wide, pair(tokens_here), pair(BLOCK_TOKENS)] + arrival_specs,
            scratch_shapes=[
                blocks,
                blocks,
                sums,
                sums,
                pltpu.SMEM((blocks_here, most_seen), jnp.int32),
                pltpu.SMEM((blocks_here,), jnp.int32),
            ],
        ),
        out_shape=[
            like(query, jnp.bfloat16),
            like(query, jnp.bfloat16),
            jax.ShapeDtypeStruct((2,) + key.shape, jnp.float32),
            like(root_pair, jnp.float32),
        ]
        + [like(a, jnp.bfloat16) for a in arrivals],
        compiler_params=pltpu.CompilerParams(vmem_limit_bytes=48 << 20),
        name=f"tree_attention_{most_seen}",
    )(parents, query, grad, key, value, root_pair, *arrivals)


def wide32(array):
    return array.astype(jnp.float32)


def run_every_block(choice, first, sent, query, key, value, output_cotangent, parents):
    blocks_here = query.shape[0] // BLOCK_TOKENS
    position = lax.axis_index("ctx")
    key_value = jnp.stack([key, value])
    (root_pair,) = spread_from_first(first)
    pieces = [passed_along(key_value, back) for back in range(HOPS, 0, -1)]
    slot_of = lambda position, back, slot: 1 + (HOPS - back) * blocks_here + slot
    plan = ((blocks_here,) * HOPS, slot_of, ())
    out, grad_q, own, root_terms, *terms = attention(
        plan, 1 + (HOPS + 1) * blocks_here, parents, query, output_cotangent, key, value,
        root_pair, pieces,
    )
    total = own + sum(
        wide32(passed_along(terms[HOPS - back], -back)) for back in range(1, HOPS + 1)
    )
    root_rows = jnp.where(position == 0, sum_to_first(root_terms)[0], 0.0)
    total = jnp.concatenate(
        [total[:, :BLOCK_TOKENS] + root_rows, total[:, BLOCK_TOKENS:]], axis=1
    ).astype(jnp.bfloat16)
    return out, grad_q, total[0], total[1]


def run_one_block(choice, first, sent, query, key, value, output_cotangent, parents):
    blocks_here = query.shape[0] // BLOCK_TOKENS
    devices = lax.axis_size("ctx")
    position = lax.axis_index("ctx")
    odd = position % 2
    swap = [(i, i ^ 1) for i in range(devices)]
    skip = [(i, i + 3) for i in range(1, devices - 3, 2)]
    mine = choice[0]
    two_back = passed_along(sent, 2)
    three_back = lax.ppermute(sent, "ctx", skip)
    root_pair, two_back, three_back = spread_from_first(first, (two_back, three_back))
    across = lax.ppermute(jnp.concatenate([two_back, sent], axis=1), "ctx", swap)

    def slot_of(position, back, slot):
        odd = lax.rem(position, 2)
        return jnp.where(back == 2, 2, jnp.where(back == 1, 3 + odd, 1 + 2 * odd))

    plan = ((1, 1, 2), slot_of, QUICK)
    out, grad_q, own, root_terms, g_three, g_two, g_across = attention(
        plan, 1 + HOPS + blocks_here, parents, query, output_cotangent, key, value, root_pair,
        [three_back, two_back, across],
    )
    from_core = lax.ppermute(g_across, "ctx", swap)
    from_three = lax.ppermute(g_three, "ctx", [(b, a) for a, b in skip])
    root_sum, from_core = sum_to_first(root_terms, (from_core,))
    merged = wide32(g_two) + wide32(from_core[:, :BLOCK_TOKENS])
    from_two = passed_along(merged.astype(jnp.bfloat16), -2)

    block = jnp.arange(blocks_here, dtype=jnp.int32)[:, None, None]
    exported = (block == mine).astype(jnp.float32)
    at_first = ((block == 0) & (position == 0)).astype(jnp.float32)

    def final(which):
        returned = wide32(from_two[which]) + wide32(from_three[which])
        returned = returned + jnp.where(odd == 0, wide32(from_core[which, BLOCK_TOKENS:]), 0.0)
        total = own[which].reshape((blocks_here, BLOCK_TOKENS, key.shape[1]))
        total = total + exported * returned[None] + at_first * root_sum[which][None]
        return total.astype(jnp.bfloat16).reshape(key.shape)

    return out, grad_q, final(0), final(1)


def local(query, key, value, output_cotangent, parents):
    choice, crowded, first, sent = exported_blocks(parents, key, value)
    return lax.cond(
        crowded[0] > 1,
        run_every_block,
        run_one_block,
        choice, first, sent, query, key, value, output_cotangent, parents,
    )


def solution(mesh):
    in_specs = (P("ctx", "tp"), P("ctx", "tp"), P("ctx", "tp"), P("ctx", "tp"), P())
    out_specs = (P("ctx", "tp"), P("ctx", "tp"), P("ctx", "tp"), P("ctx", "tp"))
    return jax.shard_map(local, mesh=mesh, in_specs=in_specs, out_specs=out_specs, check_vma=False)
```

```python
import functools
import math

import jax
import jax.numpy as jnp
from jax import lax
from jax.experimental import pallas as pl
from jax.experimental.pallas import tpu as pltpu
from jax.sharding import PartitionSpec as P

HEAD_WIDTH = 128
BLOCK_TOKENS = 128
HOPS = 3
LAYER = 4
SUB_HEADS = 2
SPAN = 2
QUICK = (2, 3, 4, 5)


def passed_along(array, by):
    devices = lax.axis_size("ctx")
    pairs = [(i, i + by) for i in range(devices) if 0 <= i + by < devices]
    return lax.ppermute(array, "ctx", pairs)


def layer_stages(layers):
    stages = []
    while layers > 1:
        fan = 4 if layers % 4 == 0 else (2 if layers % 2 == 0 else layers)
        layers //= fan
        stages.append((layers, fan))
    return stages


def spread_from_first(held, after=()):
    devices = lax.axis_size("ctx")
    position = lax.axis_index("ctx")
    layers = devices // LAYER
    layer = position // LAYER
    for stride, fan in layer_stages(layers):
        bases = range(0, layers, stride * fan)
        arrived = [
            lax.ppermute(held, "ctx", [(b * LAYER, (b + j * stride) * LAYER) for b in bases])
            for j in range(1, fan)
        ]
        held, *arrived = lax.optimization_barrier((held, *arrived))
        for j, piece in enumerate(arrived, 1):
            here = (position % LAYER == 0) & (layer % (stride * fan) == j * stride)
            held = jnp.where(here, piece, held)
    after = list(after)
    if after:
        held, after[0] = lax.optimization_barrier((held, after[0]))
    for step in (2, 1):
        if step == 1:
            held, *after = lax.optimization_barrier((held, *after))
        pairs = [(i, i + step) for i in range(0, devices, 2 * step)]
        here = (position % (2 * step)) == step
        held = jnp.where(here, lax.ppermute(held, "ctx", pairs), held)
    return (held, *after)


def sum_to_first(total, after=()):
    devices = lax.axis_size("ctx")
    layers = devices // LAYER
    home = lambda layer: layer * LAYER + (2 if layer else 0)
    stages = [[[(i + 1, i) for i in range(0, devices, 2)]]]
    stages.append([[(home(l) ^ 2, home(l)) for l in range(layers)]])
    for stride, fan in reversed(layer_stages(layers)):
        bases = range(0, layers, stride * fan)
        stages.append(
            [[(home(b + j * stride), home(b)) for b in bases] for j in range(1, fan)]
        )
    for at, stage in enumerate(stages):
        sent = total.astype(jnp.bfloat16)
        arrived = [lax.ppermute(sent, "ctx", pairs) for pairs in stage]
        if at == 1:
            arrived[0], *after = lax.optimization_barrier((arrived[0], *after))
        for piece in arrived:
            total = total + piece.astype(jnp.float32)
    return (total, *after)


def export_kernel(
    blocks_here, parents_ref, k_ref, v_ref, choice_ref, crowded_ref, first_ref, sent_ref,
    reach_ref, choices_ref
):
    block_count = parents_ref.shape[0]
    for b in range(block_count):
        reach_ref[b] = jnp.int32(b // blocks_here)
    crowded = jnp.int32(0)
    for device in reversed(range(block_count // blocks_here)):
        count = jnp.int32(0)
        choice = jnp.int32(0)
        for slot in reversed(range(blocks_here)):
            block = device * blocks_here + slot
            if block == 0:
                continue
            last = reach_ref[block]
            up = parents_ref[block]
            reach_ref[up] = jnp.maximum(reach_ref[up], last)
            read = last > device
            count = count + read.astype(jnp.int32)
            choice = jnp.where(read, slot, choice)
        choices_ref[device] = choice
        crowded = jnp.maximum(crowded, count)
    crowded_ref[0] = crowded
    mine = choices_ref[lax.axis_index("ctx")]
    choice_ref[0] = mine
    rows = pl.ds(pl.multiple_of(mine * BLOCK_TOKENS, BLOCK_TOKENS), BLOCK_TOKENS)
    for which, ref in enumerate((k_ref, v_ref)):
        first_ref[which] = ref[:BLOCK_TOKENS]
        sent_ref[which] = ref[rows]


def exported_blocks(parents, key, value):
    blocks_here = key.shape[0] // BLOCK_TOKENS
    block_count = parents.shape[0]
    smem = pl.BlockSpec(memory_space=pltpu.SMEM)
    vmem = pl.BlockSpec(memory_space=pltpu.VMEM)
    pair = jax.ShapeDtypeStruct((2, BLOCK_TOKENS, key.shape[1]), key.dtype)
    return pl.pallas_call(
        functools.partial(export_kernel, blocks_here),
        out_shape=[
            jax.ShapeDtypeStruct((1,), jnp.int32),
            jax.ShapeDtypeStruct((1,), jnp.int32),
            pair,
            pair,
        ],
        in_specs=[smem, vmem, vmem],
        out_specs=[smem, smem, vmem, vmem],
        scratch_shapes=[
            pltpu.SMEM((block_count,), jnp.int32),
            pltpu.SMEM((block_count // blocks_here,), jnp.int32),
        ],
        name="exported",
    )(parents, key, value)


NT = (((1,), (1,)), ((), ()))
NN = (((1,), (0,)), ((), ()))
TN = (((0,), (0,)), ((), ()))


def dot(a, b, dims):
    return lax.dot_general(a, b, dims, preferred_element_type=jnp.float32)


def attention_kernel(
    plan, blocks_here, heads_per_group, span, parents_ref, q_ref, do_ref, k_own, v_own, root_ref, *rest
):
    held_counts, slot_of, quick_counts = plan
    arrivals = rest[: len(held_counts)]
    (out_ref, gq_ref, gown_ref, groot_ref) = rest[len(held_counts) : len(held_counts) + 4]
    departures = rest[len(held_counts) + 4 : 2 * len(held_counts) + 4]
    k_all, v_all, gk_acc, gv_acc, slots, counts = rest[2 * len(held_counts) + 4 :]
    own_base = 1 + sum(held_counts)
    scale = 1.0 / math.sqrt(HEAD_WIDTH)
    log2e = math.log2(math.e)
    rows = SUB_HEADS * BLOCK_TOKENS
    groups = [slice(g * HEAD_WIDTH, (g + 1) * HEAD_WIDTH) for g in range(span)]
    most_seen = slots.shape[1]

    @pl.when(pl.program_id(0) == 0)
    def _():
        position = lax.axis_index("ctx")
        for qb in range(blocks_here):
            own = position * blocks_here + qb
            slots[qb, 0] = 0

            def climb(step, state):
                current, count = state
                current = parents_ref[current]
                device = lax.div(current, blocks_here)
                slot = lax.rem(current, blocks_here)
                back = position - device
                where_held = jnp.where(back == 0, own_base + slot, slot_of(position, back, slot))
                seen = (current > 0) & (back <= HOPS)

                @pl.when(seen)
                def _():
                    slots[qb, count] = where_held

                return current, count + seen.astype(jnp.int32)

            _, count = lax.fori_loop(
                0, (HOPS + 1) * blocks_here, climb, (own, jnp.int32(1))
            )

            @pl.when(own > 0)
            def _():
                slots[qb, count] = own_base + qb

            counts[qb] = jnp.where(own > 0, count + 1, 1)

    for g, cols in enumerate(groups):
        k_all[g, 0] = root_ref[0, :, cols]
        v_all[g, 0] = root_ref[1, :, cols]
        at = 1
        for arrival, count in zip(arrivals, held_counts):
            for e in range(count):
                part = slice(e * BLOCK_TOKENS, (e + 1) * BLOCK_TOKENS)
                k_all[g, at] = arrival[0, part, cols]
                v_all[g, at] = arrival[1, part, cols]
                at += 1
        for b in range(blocks_here):
            part = slice(b * BLOCK_TOKENS, (b + 1) * BLOCK_TOKENS)
            k_all[g, own_base + b] = k_own[part, cols]
            v_all[g, own_base + b] = v_own[part, cols]
    gk_acc[...] = jnp.zeros_like(gk_acc)
    gv_acc[...] = jnp.zeros_like(gv_acc)

    def run_block(qb, seen):
        held = [slots[qb, j] for j in range(seen)]
        tokens = pl.ds(pl.multiple_of(qb * BLOCK_TOKENS, BLOCK_TOKENS), BLOCK_TOKENS)
        quick = seen in quick_counts
        chunk_heads = span * heads_per_group if quick else SUB_HEADS
        skew = 1 if quick else 0
        split = lambda wide: [
            wide[:, j * BLOCK_TOKENS : (j + 1) * BLOCK_TOKENS] for j in range(seen)
        ]

        def run_chunk(chunk):
            def load(ref, sub):
                return jnp.concatenate([ref[tokens, c] for c in columns(sub)], axis=0)

            def columns(sub):
                heads = [chunk * chunk_heads + sub * SUB_HEADS + h for h in range(SUB_HEADS)]
                return [pl.ds(pl.multiple_of(h * HEAD_WIDTH, HEAD_WIDTH), HEAD_WIDTH) for h in heads]

            def group_of(sub):
                return (chunk * chunk_heads + sub * SUB_HEADS) // heads_per_group

            def blocks(ref, sub):
                return jnp.concatenate([ref[group_of(sub), s] for s in held], axis=0)

            def first(sub):
                q, do = load(q_ref, sub), load(do_ref, sub)
                return dot(q, blocks(k_all, sub), NT), dot(do, blocks(v_all, sub), NT)

            def second(sub, scores, gprobs):
                scores = split(scores)
                token = lax.broadcasted_iota(jnp.int32, (rows, BLOCK_TOKENS), 0) % BLOCK_TOKENS
                other = lax.broadcasted_iota(jnp.int32, (rows, BLOCK_TOKENS), 1)
                scores[-1] = jnp.where(other <= token, scores[-1], -jnp.inf)
                top = functools.reduce(jnp.maximum, scores)
                top = jnp.max(top, axis=1, keepdims=True) * (scale * log2e)
                raised = [jnp.exp2(s * (scale * log2e) - top) for s in scores]
                total = jnp.sum(functools.reduce(jnp.add, raised), axis=1, keepdims=True)
                inverse = 1.0 / total
                probs = [r * inverse for r in raised]
                weights = jnp.concatenate([p.astype(jnp.bfloat16) for p in probs], axis=1)
                attended = dot(weights, blocks(v_all, sub), NN).astype(jnp.bfloat16)
                for h, c in enumerate(columns(sub)):
                    out_ref[tokens, c] = attended[h * BLOCK_TOKENS : (h + 1) * BLOCK_TOKENS]
                return probs, weights, attended, gprobs

            def third(sub, probs, weights, attended, gprobs):
                q, do = load(q_ref, sub), load(do_ref, sub)
                delta = jnp.sum(
                    do.astype(jnp.float32) * attended.astype(jnp.float32), axis=1, keepdims=True
                )
                dscores = jnp.concatenate(
                    [(p * (g - delta)).astype(jnp.bfloat16) for p, g in zip(probs, split(gprobs))],
                    axis=1,
                )
                grad_q = (dot(dscores, blocks(k_all, sub), NN) * scale).astype(jnp.bfloat16)
                for h, c in enumerate(columns(sub)):
                    gq_ref[tokens, c] = grad_q[h * BLOCK_TOKENS : (h + 1) * BLOCK_TOKENS]
                gk = split(dot(q, dscores, TN))
                gv = split(dot(do, weights, TN))
                for s, x, y in zip(held, gk, gv):
                    gk_acc[group_of(sub), s] += x
                    gv_acc[group_of(sub), s] += y

            subs = chunk_heads // SUB_HEADS
            one, two = {}, {}
            for turn in range(subs + 2 * skew):
                if turn < subs:
                    one[turn] = first(turn)
                if 0 <= turn - skew < subs:
                    two[turn - skew] = second(turn - skew, *one.pop(turn - skew))
                if 0 <= turn - 2 * skew < subs:
                    third(turn - 2 * skew, *two.pop(turn - 2 * skew))

        if quick:
            run_chunk(0)
        else:
            pl.loop(0, span * heads_per_group // SUB_HEADS)(run_chunk)

    @pl.loop(0, blocks_here)
    def _(qb):
        seen_here = counts[qb]
        for seen in range(1, most_seen + 1):
            pl.when(seen_here == seen)(functools.partial(run_block, qb, seen))

    for g, cols in enumerate(groups):

        def grads(slot):
            return (gk_acc[g, slot] * scale).T, gv_acc[g, slot].T

        for b in range(blocks_here):
            part = slice(b * BLOCK_TOKENS, (b + 1) * BLOCK_TOKENS)
            gown_ref[0, part, cols], gown_ref[1, part, cols] = grads(own_base + b)
        groot_ref[0, :, cols], groot_ref[1, :, cols] = grads(0)
        at = 1
        for departure, count in zip(departures, held_counts):
            for e in range(count):
                part = slice(e * BLOCK_TOKENS, (e + 1) * BLOCK_TOKENS)
                gk, gv = grads(at)
                departure[0, part, cols] = gk.astype(jnp.bfloat16)
                departure[1, part, cols] = gv.astype(jnp.bfloat16)
                at += 1


def attention(plan, most_seen, parents, query, grad, key, value, root_pair, arrivals):
    tokens_here = query.shape[0]
    blocks_here = tokens_here // BLOCK_TOKENS
    groups = key.shape[1] // HEAD_WIDTH
    heads_per_group = query.shape[1] // HEAD_WIDTH // groups
    span = SPAN if groups % SPAN == 0 else 1
    width = span * HEAD_WIDTH
    wide = pl.BlockSpec((tokens_here, heads_per_group * width), lambda g, _: (0, g))
    narrow = pl.BlockSpec((tokens_here, width), lambda g, _: (0, g))
    pair = lambda rows: pl.BlockSpec((2, rows, width), lambda g, _: (0, 0, g))
    arrival_specs = [pair(a.shape[1]) for a in arrivals]
    slot_count = 1 + sum(plan[0]) + blocks_here
    like = lambda array, kind: jax.ShapeDtypeStruct(array.shape, kind)
    blocks = pltpu.VMEM((span, slot_count, BLOCK_TOKENS, HEAD_WIDTH), jnp.bfloat16)
    sums = pltpu.VMEM((span, slot_count, HEAD_WIDTH, BLOCK_TOKENS), jnp.float32)
    return pl.pallas_call(
        functools.partial(attention_kernel, plan, blocks_here, heads_per_group, span),
        grid_spec=pltpu.PrefetchScalarGridSpec(
            num_scalar_prefetch=1,
            grid=(groups // span,),
            in_specs=[wide, wide, narrow, narrow, pair(BLOCK_TOKENS)] + arrival_specs,
            out_specs=[wide, wide, pair(tokens_here), pair(BLOCK_TOKENS)] + arrival_specs,
            scratch_shapes=[
                blocks,
                blocks,
                sums,
                sums,
                pltpu.SMEM((blocks_here, most_seen), jnp.int32),
                pltpu.SMEM((blocks_here,), jnp.int32),
            ],
        ),
        out_shape=[
            like(query, jnp.bfloat16),
            like(query, jnp.bfloat16),
            jax.ShapeDtypeStruct((2,) + key.shape, jnp.float32),
            like(root_pair, jnp.float32),
        ]
        + [like(a, jnp.bfloat16) for a in arrivals],
        compiler_params=pltpu.CompilerParams(vmem_limit_bytes=48 << 20),
        name=f"tree_attention_{most_seen}",
    )(parents, query, grad, key, value, root_pair, *arrivals)


def wide32(array):
    return array.astype(jnp.float32)


def run_every_block(choice, first, sent, query, key, value, output_cotangent, parents):
    blocks_here = query.shape[0] // BLOCK_TOKENS
    position = lax.axis_index("ctx")
    key_value = jnp.stack([key, value])
    (root_pair,) = spread_from_first(first)
    pieces = [passed_along(key_value, back) for back in range(HOPS, 0, -1)]
    slot_of = lambda position, back, slot: 1 + (HOPS - back) * blocks_here + slot
    plan = ((blocks_here,) * HOPS, slot_of, ())
    out, grad_q, own, root_terms, *terms = attention(
        plan, 1 + (HOPS + 1) * blocks_here, parents, query, output_cotangent, key, value,
        root_pair, pieces,
    )
    total = own + sum(
        wide32(passed_along(terms[HOPS - back], -back)) for back in range(1, HOPS + 1)
    )
    root_rows = jnp.where(position == 0, sum_to_first(root_terms)[0], 0.0)
    total = jnp.concatenate(
        [total[:, :BLOCK_TOKENS] + root_rows, total[:, BLOCK_TOKENS:]], axis=1
    ).astype(jnp.bfloat16)
    return out, grad_q, total[0], total[1]


def run_one_block(choice, first, sent, query, key, value, output_cotangent, parents):
    blocks_here = query.shape[0] // BLOCK_TOKENS
    devices = lax.axis_size("ctx")
    position = lax.axis_index("ctx")
    odd = position % 2
    swap = [(i, i ^ 1) for i in range(devices)]
    skip = [(i, i + 3) for i in range(1, devices - 3, 2)]
    mine = choice[0]
    two_back = passed_along(sent, 2)
    three_back = lax.ppermute(sent, "ctx", skip)
    root_pair, two_back, three_back = spread_from_first(first, (two_back, three_back))
    across = lax.ppermute(jnp.concatenate([two_back, sent], axis=1), "ctx", swap)

    def slot_of(position, back, slot):
        odd = lax.rem(position, 2)
        return jnp.where(back == 2, 2, jnp.where(back == 1, 3 + odd, 1 + 2 * odd))

    plan = ((1, 1, 2), slot_of, QUICK)
    out, grad_q, own, root_terms, g_three, g_two, g_across = attention(
        plan, 1 + HOPS + blocks_here, parents, query, output_cotangent, key, value, root_pair,
        [three_back, two_back, across],
    )
    from_core = lax.ppermute(g_across, "ctx", swap)
    from_three = lax.ppermute(g_three, "ctx", [(b, a) for a, b in skip])
    root_sum, from_core = sum_to_first(root_terms, (from_core,))
    merged = wide32(g_two) + wide32(from_core[:, :BLOCK_TOKENS])
    from_two = passed_along(merged.astype(jnp.bfloat16), -2)

    block = jnp.arange(blocks_here, dtype=jnp.int32)[:, None, None]
    exported = (block == mine).astype(jnp.float32)
    at_first = ((block == 0) & (position == 0)).astype(jnp.float32)

    def final(which):
        returned = wide32(from_two[which]) + wide32(from_three[which])
        returned = returned + jnp.where(odd == 0, wide32(from_core[which, BLOCK_TOKENS:]), 0.0)
        total = own[which].reshape((blocks_here, BLOCK_TOKENS, key.shape[1]))
        total = total + exported * returned[None] + at_first * root_sum[which][None]
        return total.astype(jnp.bfloat16).reshape(key.shape)

    return out, grad_q, final(0), final(1)


def local(query, key, value, output_cotangent, parents):
    choice, crowded, first, sent = exported_blocks(parents, key, value)
    return lax.cond(
        crowded[0] > 1,
        run_every_block,
        run_one_block,
        choice, first, sent, query, key, value, output_cotangent, parents,
    )


def solution(mesh):
    in_specs = (P("ctx", "tp"), P("ctx", "tp"), P("ctx", "tp"), P("ctx", "tp"), P())
    out_specs = (P("ctx", "tp"), P("ctx", "tp"), P("ctx", "tp"), P("ctx", "tp"))
    return jax.shard_map(local, mesh=mesh, in_specs=in_specs, out_specs=out_specs, check_vma=False)
```
